32 devices in a mesh: dp: 16 (over z, x, core), tensor: 2 (over y).
Axes of the slice: x: 2, y: 2, z: 4, core: 2. Of those that a mesh axis runs over, the one named last changes fastest.
Arguments:
- tokens: bfloat16 [64, 512, 768], P('dp', 'tensor'), may hold values from -6 to 6
- counts: int32 [16], P('dp'), may hold values from 2 to 4, as said below
- query_key_value_weight: bfloat16 [768, 3, 768], P(None, None, 'tensor'), may hold values from -0.21875 to 0.21875
- qkv_bias: bfloat16 [3, 768], P(None, 'tensor'), may hold values from -3 to 3
- attention_output_weight: bfloat16 [768, 768], P('tensor'), may hold values from -1.75 to 1.75
- out_bias: bfloat16 [768], replicated, may hold values from -3 to 3
- up_projection_weight: bfloat16 [768, 3072], P(None, 'tensor'), may hold values from -0.21875 to 0.21875
- in_bias: bfloat16 [3072], P('tensor'), may hold values from -3 to 3
- down_projection_weight: bfloat16 [3072, 768], P('tensor'), may hold values from -0.15625 to 0.15625
- back_bias: bfloat16 [768], replicated, may hold values from -3 to 3
- project: bfloat16 [256, 512], replicated, may hold values from -0.25 to 0.25
- gain_one: bfloat16 [768], replicated, may hold values from 0.5 to 1.5
- shift_one: bfloat16 [768], replicated, may hold values from -3 to 3
- gain_two: bfloat16 [768], replicated, may hold values from 0.5 to 1.5
- shift_two: bfloat16 [768], replicated, may hold values from -3 to 3
- cotangent: bfloat16 [64, 512, 768], P('dp', 'tensor'), may hold values from -6 to 6
Outputs:
- output: bfloat16 [64, 512, 768], P('dp', 'tensor')
- input_grad: float32 [64, 512, 768], P('dp', 'tensor')
- qkv_weight_grad: float32 [768, 3, 768], P(None, None, 'tensor')
- qkv_bias_grad: float32 [3, 768], P(None, 'tensor')
- attention_output_gradient: float32 [768, 768], P('tensor')
- out_bias_grad: float32 [768], replicated
- up_projection_gradient: float32 [768, 3072], P(None, 'tensor')
- in_bias_grad: float32 [3072], P('tensor')
- down_projection_gradient: float32 [3072, 768], P('tensor')
- back_bias_grad: float32 [768], replicated
- project_grad: float32 [256, 512], replicated
- gain_one_grad: float32 [768], replicated
- shift_one_grad: float32 [768], replicated
- gain_two_grad: float32 [768], replicated
- shift_two_grad: float32 [768], replicated
The draws below stay inside these ranges and needn't reach their ends.
Inputs may be any that keep to these rules, and one draw needn't show every extreme that they name: counts[g] is the number of live sequences of group g, the first counts[g] slots of the group; some group has all 4 slots live in every draw.
All inputs are finite; a program needn't handle non-finite values.
Results may differ from the reference program's by a relative error of at most 0.018.
Values may be sent and summed in bfloat16 or wider, within the bound.
No kernel may reach another device: no remote copies, remote signals or barrier semaphores. Data moves between devices by JAX's collectives and lax.ppermute only.
A program may use at most 192 MiB of HBM per device.

```python
import jax
import jax.numpy as jnp
from jax import lax

D = 768
H = 12
HD = 64
FF = 3072
KP = 256
L = 512
SLOTS = 4
GROUPS = 16
SEQS = 64


def draw_counts(key, part):
    first_key, second_key = jax.random.split(jax.random.fold_in(key, 7))
    drawn = jax.random.randint(first_key, (GROUPS,), (SLOTS + 1) // 2, SLOTS + 1)
    fullest = jax.random.randint(second_key, (), 0, GROUPS)
    return drawn.at[fullest].set(SLOTS).astype(jnp.int32)


def block_scale(own_key, shape, shards, least, top_value):
    def one(dim, blocks):
        steps = jax.random.uniform(jax.random.fold_in(jax.random.fold_in(own_key, 6), dim), (blocks,), jnp.float32, least / len(shards), top_value / len(shards))
        return jnp.repeat(jnp.exp(steps), shape[dim] // blocks).reshape((-1,) + (1,) * (len(shape) - dim - 1))

    level = one(*shards[0])
    for cut in shards[1:]:
        level = level * one(*cut)
    return level


def bell_draw(own_key, dims, width, bound, pieces=(), kind=jnp.bfloat16):
    factor_of = block_scale(own_key, dims, pieces, -0.22, 0.18) if pieces else 1.0
    values = jax.random.normal(own_key, dims, jnp.float32) * width * factor_of
    return jnp.minimum(jnp.maximum(values, -bound), bound).astype(kind)


def setup_inputs(seed: int = 0) -> dict:
    keys = jax.random.split(jax.random.key(seed), 17)
    tokens = bell_draw(keys[0], (SEQS, L, D), 1.0, 6.0, ((0, 16), (1, 2)))
    counts = draw_counts(jax.random.fold_in(keys[16], 71), 0)
    query_key_value_weight = bell_draw(keys[2], (D, 3, D), D ** -0.5, 0.21875, ((2, 2),))
    qkv_bias = bell_draw(keys[3], (3, D), 0.3, 3.0, ((1, 2),))
    attention_output_weight = bell_draw(keys[4], (D, D), (D // 64) ** -0.5, 1.75, ((0, 2),))
    out_bias = bell_draw(keys[5], (D,), 0.5, 3.0)
    up_projection_weight = bell_draw(keys[6], (D, FF), D ** -0.5, 0.21875, ((1, 2),))
    in_bias = bell_draw(keys[7], (FF,), 0.5, 3.0, ((0, 2),))
    down_projection_weight = bell_draw(keys[8], (FF, D), (FF // 2) ** -0.5, 0.15625, ((0, 2),))
    back_bias = bell_draw(keys[9], (D,), 0.5, 3.0)
    project = bell_draw(keys[10], (KP, L), L ** -0.5, 0.25)
    gain_one = jnp.clip(1.0 + 0.1 * jax.random.normal(keys[11], (D,), jnp.float32), 0.5, 1.5).astype(jnp.bfloat16)
    shift_one = bell_draw(keys[12], (D,), 0.5, 3.0)
    gain_two = jnp.clip(1.0 + 0.1 * jax.random.normal(keys[13], (D,), jnp.float32), 0.5, 1.5).astype(jnp.bfloat16)
    shift_two = bell_draw(keys[14], (D,), 0.5, 3.0)
    cotangent = bell_draw(keys[15], (SEQS, L, D), 1.0, 6.0, ((0, 16), (1, 2)))
    return dict(tokens=tokens, counts=counts, query_key_value_weight=query_key_value_weight, qkv_bias=qkv_bias, attention_output_weight=attention_output_weight, out_bias=out_bias, up_projection_weight=up_projection_weight, in_bias=in_bias, down_projection_weight=down_projection_weight, back_bias=back_bias, project=project, gain_one=gain_one, shift_one=shift_one, gain_two=gain_two, shift_two=shift_two, cotangent=cotangent)


EPSILON = 1e-05
HIGH = lax.Precision.HIGHEST

@jax.custom_vjp
def low(v):
    return lax.optimization_barrier(v.astype(jnp.bfloat16)).astype(jnp.float32)

@jax.custom_vjp
def low_back(v):
    return v

def low_keep(v):
    return (low(v), None)

def low_pass(kept, grad):
    return (grad,)

def back_keep(v):
    return (v, None)

def back_low(kept, grad):
    return (low(grad),)
low.defvjp(low_keep, low_pass)
low_back.defvjp(back_keep, back_low)

def layer_norm(values, gain, shift):
    row_mean = lax.optimization_barrier(jnp.mean(values, -1, keepdims=True))
    centred = values - row_mean
    variance = lax.optimization_barrier(jnp.mean(centred * centred, -1, keepdims=True))
    return centred * lax.rsqrt(variance + EPSILON) * gain + shift

def group_layer(weights, tokens_group, live_group):
    query_key_value_weight, qkv_bias, attention_output_weight, out_bias, up_projection_weight, in_bias, down_projection_weight, back_bias, project, gain_one, shift_one, gain_two, shift_two = weights
    rows = tokens_group.reshape(SLOTS * L, D)
    mixed = jnp.dot(rows, query_key_value_weight.reshape(D, 3 * D), precision=HIGH) + qkv_bias.reshape(3 * D)
    mixed = mixed.reshape(SLOTS, L, 3, H, HD)
    query_rows = low_back(low(mixed[:, :, 0]))
    key_rows = low_back(low(mixed[:, :, 1]))
    value_rows = low_back(low(mixed[:, :, 2]))
    keys_short = low_back(low(jnp.einsum('jl,slhe->sjhe', project, key_rows, precision=HIGH)))
    values_short = low_back(low(jnp.einsum('jl,slhe->sjhe', project, value_rows, precision=HIGH)))
    scores = low_back(jnp.einsum('slhe,sjhe->shlj', query_rows, keys_short, precision=HIGH) * HD ** (-0.5))
    softmaxed = low(jax.nn.softmax(scores, axis=-1))
    attended_values = jnp.einsum('shlj,sjhe->slhe', softmaxed, values_short, precision=HIGH)
    attended_values = low_back(low(attended_values)).reshape(SLOTS * L, D)
    attn_sum = low_back(jnp.dot(attended_values, attention_output_weight, precision=HIGH)) + out_bias
    first_out = layer_norm(rows + attn_sum, gain_one, shift_one)
    inner_act = low_back(jnp.dot(low(first_out), up_projection_weight, precision=HIGH) + in_bias)
    hidden_state = low(jax.nn.gelu(inner_act, approximate=False))
    ffn_sum = low_back(jnp.dot(hidden_state, down_projection_weight, precision=HIGH)) + back_bias
    second = layer_norm(first_out + ffn_sum, gain_two, shift_two)
    return second.reshape(SLOTS, L, D) * live_group[:, None, None]

def reference(tokens, counts, query_key_value_weight, qkv_bias, attention_output_weight, out_bias, up_projection_weight, in_bias, down_projection_weight, back_bias, project, gain_one, shift_one, gain_two, shift_two, cotangent):
    live_slots = (jnp.arange(SLOTS)[None, :] < counts[:, None]).astype(jnp.float32)
    floats = tuple((w.astype(jnp.float32) for w in (query_key_value_weight, qkv_bias, attention_output_weight, out_bias, up_projection_weight, in_bias, down_projection_weight, back_bias, project, gain_one, shift_one, gain_two, shift_two)))
    checked_layer = jax.checkpoint(group_layer)

    def forward(tokens_float, weights):
        grouped = tokens_float.reshape(GROUPS, SLOTS, L, D)
        outcome = lax.map(lambda group_pair: checked_layer(weights, group_pair[0], group_pair[1]), (grouped, live_slots))
        return outcome.reshape(SEQS, L, D)
    result, pullback = jax.vjp(forward, tokens.astype(jnp.float32), floats)
    grad_tokens, grad_weights = pullback(cotangent.astype(jnp.float32))
    g_qkv_weight, g_qkv_bias, g_out_weight, g_out_bias, g_in_weight, g_in_bias, g_back_weight, g_back_bias, g_project, g_gain_one, g_shift_one, g_gain_two, g_shift_two = grad_weights
    return (result.astype(jnp.bfloat16), grad_tokens, g_qkv_weight, g_qkv_bias, g_out_weight, g_out_bias, g_in_weight, g_in_bias, g_back_weight, g_back_bias, g_project, g_gain_one, g_shift_one, g_gain_two, g_shift_two)
```

```python
import functools

import jax
import jax.numpy as jnp
from jax import lax
from jax.experimental import pallas as pl
from jax.experimental.pallas import tpu as pltpu
from jax.sharding import PartitionSpec as P

HD = 64
EPSILON = 1e-05
F32 = jnp.float32
BF16 = jnp.bfloat16


def mm(a, b, dims, out=F32):
    return lax.dot_general(a, b, (dims, ((), ())), preferred_element_type=F32).astype(out)


def norm_rows(values, gain, shift):
    row_mean = jnp.mean(values, -1, keepdims=True)
    centred = values - row_mean
    inverse = lax.rsqrt(jnp.mean(centred * centred, -1, keepdims=True) + EPSILON)
    normal = centred * inverse
    return (normal * gain + shift, normal, inverse)


def norm_back(grad_out, normal, inverse, gain):
    scaled = grad_out * gain
    return inverse * (
        scaled
        - jnp.mean(scaled, -1, keepdims=True)
        - normal * jnp.mean(scaled * normal, -1, keepdims=True)
    )


def head_masks(shape):
    lane = lax.broadcasted_iota(jnp.int32, shape, 1)
    return [(lane // HD) == h for h in range(shape[1] // HD)]


def soft(q, ks_masked, scale):
    s = mm(ks_masked, q, ((1,), (1,)))
    top = jnp.max(s, 0, keepdims=True)
    e = jnp.exp((s - top) * scale)
    return e * (1.0 / jnp.sum(e, 0, keepdims=True))


def attend_kernel(q_ref, ks_ref, vs_ref, o_ref):
    q, ks, vs = q_ref[...], ks_ref[...], vs_ref[...]
    scale = HD ** (-0.5)
    zero = jnp.zeros_like(ks)
    total = None
    for mask in head_masks(ks.shape):
        p = soft(q, jnp.where(mask, ks, zero), scale).astype(BF16)
        part = mm(jnp.where(mask, vs, zero), p, ((0,), (0,)))
        total = part if total is None else total + part
    o_ref[...] = total.T.astype(BF16)


def attend_back_kernel(q_ref, ks_ref, vs_ref, g_ref, dq_ref, dk_ref, dv_ref):
    q, ks, vs, g = q_ref[...], ks_ref[...], vs_ref[...], g_ref[...]
    scale = HD ** (-0.5)
    zero = jnp.zeros_like(ks)
    dq, dk, dv = None, None, None
    for mask in head_masks(ks.shape):
        ksm = jnp.where(mask, ks, zero)
        p = soft(q, ksm, scale)
        dv_h = mm(p.astype(BF16), g, ((1,), (0,)))
        gp = mm(jnp.where(mask, vs, zero), g, ((1,), (1,)))
        t = p * gp
        ds = (t - p * jnp.sum(t, 0, keepdims=True)).astype(BF16)
        dk_h = mm(ds, q, ((1,), (0,)))
        dq_h = mm(ksm, ds, ((0,), (0,)))
        if dq is None:
            dq, dk, dv = dq_h, dk_h, dv_h
        else:
            dq = dq + dq_h
            dk = jnp.where(mask, dk_h, dk)
            dv = jnp.where(mask, dv_h, dv)
    dq_ref[...] = (dq * scale).T.astype(BF16)
    dk_ref[...] = (dk * scale).astype(BF16)
    dv_ref[...] = dv.astype(BF16)


def attend(q, ks, vs, seqs):
    rows, width = q.shape
    length, short = rows // seqs, ks.shape[0] // seqs
    pair = min(2 * HD, width)
    spec = lambda n: pl.BlockSpec((n, pair), lambda s, p: (s, p))
    heads = width // HD
    return pl.pallas_call(
        attend_kernel,
        grid=(seqs, width // pair),
        in_specs=[spec(length), spec(short), spec(short)],
        out_specs=spec(length),
        out_shape=jax.ShapeDtypeStruct(q.shape, BF16),
        cost_estimate=pl.CostEstimate(
            flops=8 * rows * short * HD * heads, bytes_accessed=8 * rows * width,
            transcendentals=rows * short * heads),
        name="attend",
    )(q, ks, vs)


def attend_back(q, ks, vs, g, seqs):
    rows, width = q.shape
    length, short = rows // seqs, ks.shape[0] // seqs
    pair = min(2 * HD, width)
    spec = lambda n: pl.BlockSpec((n, pair), lambda s, p: (s, p))
    heads = width // HD
    return pl.pallas_call(
        attend_back_kernel,
        grid=(seqs, width // pair),
        in_specs=[spec(length), spec(short), spec(short), spec(length)],
        out_specs=[spec(length), spec(short), spec(short)],
        out_shape=[jax.ShapeDtypeStruct(a.shape, BF16) for a in (q, ks, vs)],
        cost_estimate=pl.CostEstimate(
            flops=20 * rows * short * HD * heads, bytes_accessed=16 * rows * width,
            transcendentals=rows * short * heads),
        name="attend_back",
    )(q, ks, vs, g)


class Links:
    def __init__(self, mesh):
        self.size = mesh.shape["dp"]
        self.bits = self.size.bit_length() - 1
        assert self.size == 1 << self.bits and mesh.shape["tensor"] == 2
        self.d = lax.axis_index("dp")
        self.t = lax.axis_index("tensor")

    def bit(self, b):
        return (self.d >> b) & 1

    def swap(self, a, b):
        return lax.ppermute(a, "dp", [(i, i ^ (1 << b)) for i in range(self.size)])

    def swap_y(self, a):
        return lax.ppermute(a, "tensor", [(0, 1), (1, 0)])


def part(a, index, count):
    n = a.shape[0] // count
    return lax.dynamic_slice_in_dim(a, index * n, n, 0)


def ordered(bit, mine, theirs):
    return jnp.where(
        bit == 0,
        jnp.concatenate([mine, theirs], 0),
        jnp.concatenate([theirs, mine], 0),
    )


def tie(a, *before):
    return lax.optimization_barrier((a,) + before)[0]


def fetch(links, own, after):
    got = links.swap_y(tie(part(own, links.bit(0), 2), after))
    return ordered(links.bit(0), got, links.swap(got, 0)), got


def halve(links, a, b):
    bit = links.bit(b)
    return part(a, bit, 2), links.swap(part(a, 1 - bit, 2), b)


def add(a, b):
    return (a.astype(F32) + b.astype(F32)).astype(BF16)


def reduce_other(links, other):
    return links.swap_y(add(*halve(links, other, 0)))


def reduce_own(links, own, from_y):
    keep, got = halve(links, own, 0)
    a = (keep.astype(F32) + got.astype(F32) + from_y.astype(F32)).astype(BF16)
    for b in range(1, links.bits):
        a = add(*halve(links, a, b))
    for b in reversed(range(1, links.bits)):
        a = ordered(links.bit(b), a, links.swap(a, b))
    return ordered(links.bit(0), a, links.swap(a, 0)).astype(F32)


def sum_all(links, a, kind):
    a = a.astype(kind)
    for b in range(links.bits):
        a = (a.astype(F32) + links.swap(a, b).astype(F32)).astype(kind)
    a = (a.astype(F32) + links.swap_y(a).astype(F32)).astype(kind)
    return a.astype(F32)


def body(
    mesh,
    tokens,
    counts,
    query_key_value_weight,
    qkv_bias,
    attention_output_weight,
    out_bias,
    up_projection_weight,
    in_bias,
    down_projection_weight,
    back_bias,
    project,
    gain_one,
    shift_one,
    gain_two,
    shift_two,
    cotangent,
):
    links = Links(mesh)
    t = links.t
    slots, half_rows, width = tokens.shape
    seqs = slots // 2
    length = 2 * half_rows
    rows = seqs * length
    short = project.shape[0]

    def whole(mine, theirs):
        return jnp.concatenate([mine, theirs], 1).reshape(rows, width)

    tokens_got = links.swap_y(part(tokens, 1 - t, 2))
    x = whole(part(tokens, t, 2), tokens_got)
    w_own = jnp.transpose(query_key_value_weight, (1, 0, 2))
    w_other, got = fetch(links, w_own.reshape(3 * width, -1), tokens_got)
    w_other = w_other.reshape(w_own.shape)
    o_own = attention_output_weight
    o_other, got = fetch(links, o_own, got)
    small_bias = jnp.concatenate([qkv_bias.reshape(-1), in_bias]).reshape(1, -1)
    small_other = links.swap_y(small_bias)[0]
    bias_own = qkv_bias
    bias_other = small_other[: qkv_bias.size].reshape(qkv_bias.shape)
    in_own = in_bias
    in_other = small_other[qkv_bias.size :]
    u_own = up_projection_weight
    u_other, got = fetch(links, u_own, got)
    d_own = down_projection_weight
    d_other, got = fetch(links, d_own, got)
    c_got = links.swap_y(tie(part(cotangent, 1 - t, 2), got))
    c = whole(part(cotangent, t, 2), c_got)

    slot = jnp.arange(seqs) + seqs * t
    live = jnp.repeat((slot < counts[0]).astype(F32), length)[:, None]
    turned = jnp.where(t == 0, project, jnp.roll(project, half_rows, 1))
    row_sums = jnp.sum(turned.astype(F32), 1)

    x3 = x.reshape(seqs, length, width)
    px = jnp.concatenate([mm(turned, x3[s], ((1,), (0,)), BF16) for s in range(seqs)], 0)
    row_sums_all = jnp.tile(row_sums, seqs)[:, None]

    def side_forward(w, bias):
        bias = bias.astype(F32)
        q = (mm(x, w[0], ((1,), (0,))) + bias[0]).astype(BF16)
        ks = (mm(px, w[1], ((1,), (0,))) + row_sums_all * bias[1]).astype(BF16)
        vs = (mm(px, w[2], ((1,), (0,))) + row_sums_all * bias[2]).astype(BF16)
        return q, ks, vs, attend(q, ks, vs, seqs)

    q_a, ks_a, vs_a, ctx_a = side_forward(w_own, bias_own)
    q_b, ks_b, vs_b, ctx_b = side_forward(w_other, bias_other)
    attention = mm(ctx_a, o_own, ((1,), (0,))) + mm(ctx_b, o_other, ((1,), (0,)))
    gain_one_f = gain_one.astype(F32)
    gain_two_f = gain_two.astype(F32)
    first_out, normal_one, inverse_one = norm_rows(
        x.astype(F32) + attention + out_bias.astype(F32), gain_one_f, shift_one.astype(F32)
    )
    first_low = first_out.astype(BF16)

    def side_ffn(u, bias):
        inner = mm(first_low, u, ((1,), (0,))) + bias.astype(F32)
        bell = 0.5 * (1.0 + lax.erf(inner * 0.7071067811865476))
        slope = bell + inner * jnp.exp(-0.5 * inner * inner) * 0.3989422804014327
        return lax.optimization_barrier(((inner * bell).astype(BF16), slope.astype(BF16)))

    hidden_a, slope_a = side_ffn(u_own, in_own)
    hidden_b, slope_b = side_ffn(u_other, in_other)
    ffn = mm(hidden_a, d_own, ((1,), (0,))) + mm(hidden_b, d_other, ((1,), (0,)))
    second, normal_two, inverse_two = norm_rows(
        first_out + ffn + back_bias.astype(F32), gain_two_f, shift_two.astype(F32)
    )
    out_rows = (second * live).astype(BF16).reshape(seqs, 2, half_rows, width)
    out_got = links.swap_y(out_rows[:, 1])
    output = ordered(t, out_rows[:, 0], out_got)

    grad_out = c.astype(F32) * live
    grad_two = norm_back(grad_out, normal_two, inverse_two, gain_two_f)
    gain_two_grad = jnp.sum(grad_out * normal_two, 0)
    shift_two_grad = jnp.sum(grad_out, 0)
    back_bias_grad = jnp.sum(grad_two, 0)
    grad_ffn = grad_two.astype(BF16)

    down_b = mm(hidden_b, grad_ffn, ((0,), (0,)), BF16)
    down_y = reduce_other(links, down_b)
    down_a = mm(hidden_a, grad_ffn, ((0,), (0,)), BF16)

    def side_inner(d, slope):
        return (mm(grad_ffn, d, ((1,), (1,))) * slope.astype(F32)).astype(BF16)

    inner_b = side_inner(d_other, slope_b)
    up_b = mm(first_low, inner_b, ((0,), (0,)), BF16)
    up_y = reduce_other(links, up_b)
    inner_a = side_inner(d_own, slope_a)
    up_a = mm(first_low, inner_a, ((0,), (0,)), BF16)
    in_grad_a = jnp.sum(inner_a.astype(F32), 0)
    in_grad_b = jnp.sum(inner_b.astype(F32), 0)
    down_grad = reduce_own(links, down_a, down_y)
    up_grad = reduce_own(links, up_a, up_y)

    grad_first = (
        grad_two + mm(inner_a, u_own, ((1,), (1,))) + mm(inner_b, u_other, ((1,), (1,)))
    )
    grad_one = norm_back(grad_first, normal_one, inverse_one, gain_one_f)
    gain_one_grad = jnp.sum(grad_first * normal_one, 0)
    shift_one_grad = jnp.sum(grad_first, 0)
    out_bias_grad = jnp.sum(grad_one, 0)
    grad_att = grad_one.astype(BF16)

    o_b = mm(ctx_b, grad_att, ((0,), (0,)), BF16)
    o_a = mm(ctx_a, grad_att, ((0,), (0,)), BF16)
    o_y = reduce_other(links, o_b)
    o_grad = reduce_own(links, o_a, o_y)

    def side_back(q, ks, vs, o, w, bias):
        g = mm(grad_att, o, ((1,), (1,)), BF16)
        dq, dk, dv = attend_back(q, ks, vs, g, seqs)
        w_grad = jnp.concatenate(
            [
                mm(x, dq, ((0,), (0,)), BF16),
                mm(px, dk, ((0,), (0,)), BF16),
                mm(px, dv, ((0,), (0,)), BF16),
            ],
            0,
        )
        dkf, dvf = dk.astype(F32), dv.astype(F32)
        b_grad = jnp.stack(
            [
                jnp.sum(dq.astype(F32), 0),
                jnp.sum(dkf * row_sums_all, 0),
                jnp.sum(dvf * row_sums_all, 0),
            ]
        )
        bias = bias.astype(F32)
        base = jnp.sum(dkf * bias[1] + dvf * bias[2], 1).reshape(seqs, short).sum(0)
        rows_grad = mm(dq, w[0], ((1,), (1,)))
        px_grad = mm(dk, w[1], ((1,), (1,))) + mm(dv, w[2], ((1,), (1,)))
        return w_grad, b_grad, base, rows_grad, px_grad

    w_b, b_b, base_b, rows_b, px_b = side_back(q_b, ks_b, vs_b, o_other, w_other, bias_other)
    w_y = reduce_other(links, w_b)
    w_a, b_a, base_a, rows_a, px_a = side_back(q_a, ks_a, vs_a, o_own, w_own, bias_own)
    w_grad = reduce_own(links, w_a, w_y)
    w_grad = jnp.transpose(w_grad.reshape(w_own.shape), (1, 0, 2))

    px_grad = (px_a + px_b).astype(BF16).reshape(seqs, short, width)
    spread = jnp.concatenate([mm(turned, px_grad[s], ((0,), (0,))) for s in range(seqs)], 0)
    in_rows = (grad_one + rows_a + rows_b + spread).reshape(seqs, 2, half_rows, width)
    in_got = links.swap_y(in_rows[:, 1].astype(BF16)).astype(F32)
    input_grad = ordered(t, in_rows[:, 0], in_got)

    project_grad = sum(mm(px_grad[s], x3[s], ((1,), (1,))) for s in range(seqs))
    project_grad = project_grad + (base_a + base_b)[:, None]
    project_grad = jnp.where(t == 0, project_grad, jnp.roll(project_grad, half_rows, 1))
    project_grad = sum_all(links, project_grad, BF16)

    def both(a, b):
        return jnp.where(t == 0, jnp.concatenate([a, b], -1), jnp.concatenate([b, a], -1))

    vectors = jnp.concatenate(
        [
            both(b_a, b_b),
            both(in_grad_a, in_grad_b).reshape(-1, width),
            jnp.stack(
                [out_bias_grad, back_bias_grad, gain_one_grad, shift_one_grad, gain_two_grad, shift_two_grad]
            ),
        ],
        0,
    )
    vectors = sum_all(links, vectors, F32)
    n_in = in_bias.shape[0]
    columns = qkv_bias.shape[1]
    qkv_bias_grad = lax.dynamic_slice_in_dim(vectors[:3], t * columns, columns, 1)
    in_rows_count = 2 * n_in // width
    in_bias_grad = lax.dynamic_slice_in_dim(
        vectors[3 : 3 + in_rows_count].reshape(-1), t * n_in, n_in, 0
    )
    rest = vectors[3 + in_rows_count :]
    return (
        output,
        input_grad,
        w_grad,
        qkv_bias_grad,
        o_grad,
        rest[0],
        up_grad,
        in_bias_grad,
        down_grad,
        rest[1],
        project_grad,
        rest[2],
        rest[3],
        rest[4],
        rest[5],
    )


def solution(mesh):
    return jax.shard_map(
        functools.partial(body, mesh),
        mesh=mesh,
        in_specs=(
            P("dp", "tensor", None),
            P("dp"),
            P(None, None, "tensor"),
            P(None, "tensor"),
            P("tensor", None),
            P(),
            P(None, "tensor"),
            P("tensor"),
            P("tensor", None),
            P(),
            P(),
            P(),
            P(),
            P(),
            P(),
            P("dp", "tensor", None),
        ),
        out_specs=(
            P("dp", "tensor", None),
            P("dp", "tensor", None),
            P(None, None, "tensor"),
            P(None, "tensor"),
            P("tensor", None),
            P(),
            P(None, "tensor"),
            P("tensor"),
            P("tensor", None),
            P(),
            P(),
            P(),
            P(),
            P(),
            P(),
        ),
        check_vma=False,
    )
```
